32 devices in a mesh: band: 4 (over y, x), slab: 8 (over z, core).
Axes of the slice: x: 2, y: 2, z: 4, core: 2. Of those that a mesh axis runs over, the one named last changes fastest.
Arguments:
- band_block: float32 [4, 2, 2, 128, 128, 128], P(None, None, None, 'band', 'slab'), may hold values from -24 to 24
- material_grid: int32 [128, 128, 128], P('slab'), may hold values from 0 to 3
- inverse_permittivity: float32 [4], replicated, may hold values from 0.077 to 1
- bloch_index: int32 [1], replicated, may hold values from 0 to 7
Outputs:
- search_block: float32 [4, 2, 2, 128, 128, 128], P(None, None, None, 'band', 'slab')
- correlation: float32 [2, 8, 8], replicated
- projected: float32 [2, 8, 8], replicated
The draws below stay inside these ranges and needn't reach their ends.
All inputs are finite; a program needn't handle non-finite values.
Results may differ from the reference program's by a relative error of at most 0.00005.
Values sent between devices are 32-bit elements; how exact they have to be, the bound alone decides.
No kernel may reach another device: no remote copies, remote signals or barrier semaphores. Data moves between devices by JAX's collectives and lax.ppermute only.
A program may use at most 192 MiB of HBM per device.

```python
import math
import jax
import jax.numpy as jnp
from jax import lax

NX = 128
NY = 128
NZ = 128
MATERIALS = 4
KPOINTS = 8
BANDS = 4
NPTS = 2097152


def signed_fraction(length):
    indices = jnp.arange(length, dtype=jnp.int32)
    signed = jnp.where(indices >= length // 2, indices - length, indices).astype(jnp.float32)
    return signed / length


def draw_band_block(key, part):
    own_key = jax.random.fold_in(key, 11)
    common_key = jax.random.fold_in(key, 12)
    grid_shape = (BANDS, 2, 2, NZ, NY, NX)
    common = jnp.clip(jax.random.normal(common_key, (1, 2, 2, NZ, NY, NX), jnp.float32), -4.0, 4.0)
    own = jnp.clip(jax.random.normal(own_key, grid_shape, jnp.float32), -4.0, 4.0)
    depth_part = signed_fraction(NZ)[:, None, None]
    height_part = signed_fraction(NY)[None, :, None]
    width_part = signed_fraction(NX)[None, None, :]
    envelope = 3.0 / (1.0 + 12.0 * (depth_part * depth_part + height_part * height_part + width_part * width_part))
    return (envelope * (own + 0.7 * common)).astype(jnp.float32)


def set_ends(drawn, key, smallest, largest):
    index_at = [jax.random.randint(jax.random.fold_in(key, axis), (), 0, length) for axis, length in enumerate(drawn.shape)]
    longest = drawn.shape.index(max(drawn.shape))
    next_to = index_at[:longest] + [(index_at[longest] + 1) % drawn.shape[longest]] + index_at[longest + 1:]
    return drawn.at[tuple(index_at)].set(smallest).at[tuple(next_to)].set(largest)


def setup_inputs(seed: int = 0) -> dict:
    key_list = jax.random.split(jax.random.key(seed), 5)
    band_block = draw_band_block(jax.random.fold_in(key_list[4], 71), 0)
    material_grid = set_ends(jax.random.randint(key_list[1], (NZ, NY, NX), 0, MATERIALS), jax.random.fold_in(key_list[1], 1), 0, MATERIALS - 1).astype(jnp.int32)
    inverse_permittivity = jnp.clip(jnp.exp(jax.random.uniform(key_list[2], (MATERIALS,), jnp.float32, math.log(0.077), math.log(1.0))), 0.077, 1.0)
    bloch_index = jax.random.randint(key_list[3], (1,), 0, KPOINTS).astype(jnp.int32)
    return dict(band_block=band_block, material_grid=material_grid, inverse_permittivity=inverse_permittivity, bloch_index=bloch_index)


HIGHEST = lax.Precision.HIGHEST

def axis_values(length, weight, fraction, offset, extent):
    indices = offset + jnp.arange(extent, dtype=jnp.int32)
    signed = jnp.where(indices >= length // 2, indices - length, indices).astype(jnp.float32)
    return 2.0 * math.pi / length * (signed + weight * fraction)

def frame(depth_wave, height_wave, width_wave):
    depth_term = depth_wave[:, None, None]
    height_term = height_wave[None, :, None]
    width_term = width_wave[None, None, :]
    planar = jnp.sqrt(width_term * width_term + height_term * height_term)
    magnitude = jnp.sqrt(planar * planar + depth_term * depth_term)
    grid_shape = magnitude.shape
    primary = [jnp.broadcast_to(height_term / planar, grid_shape), jnp.broadcast_to(-width_term / planar, grid_shape), jnp.zeros(grid_shape, magnitude.dtype)]
    secondary = [width_term * depth_term / (magnitude * planar), height_term * depth_term / (magnitude * planar), jnp.broadcast_to(-planar / magnitude, grid_shape)]
    return (primary, secondary, magnitude)

def curl_field(block, primary, secondary, magnitude):
    first_comp = block[:, 0]
    second_comp = block[:, 1]
    parts = [magnitude * (first_comp * secondary[component] - second_comp * primary[component]) for component in range(3)]
    return jnp.stack(parts, axis=1).reshape((-1,) + first_comp.shape[1:])

def project_back(spectrum, primary, secondary, magnitude, band_count):
    grouped = spectrum.reshape((band_count, 3) + spectrum.shape[1:])
    along_second = grouped[:, 0] * secondary[0] + grouped[:, 1] * secondary[1] + grouped[:, 2] * secondary[2]
    along_primary = grouped[:, 0] * primary[0] + grouped[:, 1] * primary[1] + grouped[:, 2] * primary[2]
    return jnp.stack([magnitude * along_second, -magnitude * along_primary], axis=1)

def operate(block, inverse_cells, primary, secondary, magnitude):

    def one_band(single):
        curled = curl_field(single[None], primary, secondary, magnitude)
        spectrum = curled[:, 0] + 1j * curled[:, 1]
        spatial = jnp.fft.ifftn(spectrum, axes=(1, 2, 3)) * inverse_cells
        returned = jnp.fft.fftn(spatial, axes=(1, 2, 3))
        values = jnp.stack([jnp.real(returned), jnp.imag(returned)], axis=1)
        return project_back(values, primary, secondary, magnitude, 1)[0]
    return lax.map(one_band, block)

def gram_parts(left, right):
    left_real = left[:, :, 0].reshape(left.shape[0], -1)
    left_imag = left[:, :, 1].reshape(left.shape[0], -1)
    right_real = right[:, :, 0].reshape(right.shape[0], -1)
    right_imag = right[:, :, 1].reshape(right.shape[0], -1)
    inner_product = lambda first_rows, second_rows: jnp.einsum('km,jm->kj', first_rows, second_rows, precision=HIGHEST)
    real_sum = inner_product(left_real, right_real) + inner_product(left_imag, right_imag)
    imag_sum = inner_product(left_real, right_imag) - inner_product(left_imag, right_real)
    return (real_sum / NPTS, imag_sum / NPTS)

def reference(band_block, material_grid, inverse_permittivity, bloch_index):
    fraction = (bloch_index[0].astype(jnp.float32) + 1.0) / KPOINTS
    primary, secondary, magnitude = frame(axis_values(NZ, 0.2, fraction, 0, NZ), axis_values(NY, 0.35, fraction, 0, NY), axis_values(NX, 0.5, fraction, 0, NX))
    inverse_cells = inverse_permittivity[material_grid]
    image = operate(band_block, inverse_cells, primary, secondary, magnitude)
    correlation_real, correlation_imag = gram_parts(band_block, band_block)
    cross_real, cross_imag = gram_parts(band_block, image)
    system = jnp.concatenate([jnp.concatenate([correlation_real, -correlation_imag], 1), jnp.concatenate([correlation_imag, correlation_real], 1)], 0)
    right_side = jnp.concatenate([cross_real, cross_imag], 0)
    solution = jnp.linalg.solve(system, right_side)
    mixing_real = solution[:BANDS]
    mixing_imag = solution[BANDS:]
    block_real = band_block[:, :, 0]
    block_imag = band_block[:, :, 1]
    combine = lambda data, mixing: jnp.einsum('iabcd,ij->jabcd', data, mixing, precision=HIGHEST)
    residual_real = image[:, :, 0] - (combine(block_real, mixing_real) - combine(block_imag, mixing_imag))
    residual_imag = image[:, :, 1] - (combine(block_real, mixing_imag) + combine(block_imag, mixing_real))
    search_block = jnp.stack([residual_real, residual_imag], axis=2) / (magnitude * magnitude + 1.0)
    search_image = operate(search_block, inverse_cells, primary, secondary, magnitude)
    stacked = jnp.concatenate([band_block, search_block], 0)
    images = jnp.concatenate([image, search_image], 0)
    full_real, full_imag = gram_parts(stacked, stacked)
    proj_real, proj_imag = gram_parts(stacked, images)
    return (search_block, jnp.stack([full_real, full_imag], 0), jnp.stack([proj_real, proj_imag], 0))
```

```python
from functools import partial
import math

import jax
import jax.numpy as jnp
from jax import lax
from jax.experimental import pallas as pl
from jax.experimental.pallas import tpu as pltpu
from jax.sharding import PartitionSpec as P

KPOINTS = 8


HIGH = lax.Precision.HIGH
HIGHEST = lax.Precision.HIGHEST


def axis_values(length, weight, fraction, offset, extent):
    indices = offset + jnp.arange(extent, dtype=jnp.int32)
    signed = jnp.where(indices >= length // 2, indices - length, indices).astype(jnp.float32)
    return 2.0 * math.pi / length * (signed + weight * fraction)


def frame(depth_wave, height_wave, width_wave):
    depth_term = depth_wave[:, None, None]
    height_term = height_wave[None, :, None]
    width_term = width_wave[None, None, :]
    planar = jnp.sqrt(width_term * width_term + height_term * height_term)
    magnitude = jnp.sqrt(planar * planar + depth_term * depth_term)
    grid_shape = magnitude.shape
    primary = [
        jnp.broadcast_to(height_term / planar, grid_shape),
        jnp.broadcast_to(-width_term / planar, grid_shape),
        jnp.zeros(grid_shape, magnitude.dtype),
    ]
    secondary = [
        width_term * depth_term / (magnitude * planar),
        height_term * depth_term / (magnitude * planar),
        -planar / magnitude,
    ]
    return (primary, secondary, magnitude)


def curl_field(block, primary, secondary, magnitude):
    first_comp = block[:, 0]
    second_comp = block[:, 1]
    return [
        magnitude * (first_comp * secondary[component] - second_comp * primary[component])
        for component in range(3)
    ]


def project_back(grouped, primary, secondary, magnitude):
    along_second = grouped[0] * secondary[0] + grouped[1] * secondary[1] + grouped[2] * secondary[2]
    along_primary = grouped[0] * primary[0] + grouped[1] * primary[1]
    return jnp.stack([magnitude * along_second, -magnitude * along_primary], axis=1)


def cell_values(material_grid, inverse_permittivity, grid_cells):
    inverse_cells = jnp.zeros(material_grid.shape, jnp.float32)
    for material in range(inverse_permittivity.shape[0]):
        inverse_cells = inverse_cells + jnp.where(
            material_grid == material, inverse_permittivity[material], 0.0
        )
    return inverse_cells / grid_cells


def transform(values, target, direction, precision=HIGHEST):
    length = values.shape[target]
    indices = jnp.arange(length, dtype=jnp.int32)
    products = indices[:, None] * indices[None, :] % length
    angles = 2.0 * math.pi / length * products.astype(jnp.float32)
    cosine = jnp.cos(angles)
    sine = direction * jnp.sin(angles)
    table = jnp.stack([jnp.stack([cosine, sine], 1), jnp.stack([-sine, cosine], 1)], 0)
    letters = "abc"
    source = letters[target - 2]
    formula = "ip" + letters + ",p" + source + "qw->iq" + letters.replace(source, "w")
    return jnp.einsum(formula, values, table, precision=precision)


def tile_sum(values):
    return jnp.sum(values.reshape((-1, 8) + values.shape[-1:]), axis=0)


def add_pairs(acc_ref, base, left, right):
    count = len(left)
    for i in range(count):
        for j in range(count):
            real_sum = None
            imag_sum = None
            for (lr, li), (rr, ri) in zip(left[i], right[j]):
                real_part = lr * rr + li * ri
                imag_part = lr * ri - li * rr
                real_sum = real_part if real_sum is None else real_sum + real_part
                imag_sum = imag_part if imag_sum is None else imag_sum + imag_part
            at = base + 2 * (i * count + j)
            acc_ref[at] += tile_sum(real_sum)
            acc_ref[at + 1] += tile_sum(imag_sum)


def load_bands(ref, at):
    return [
        [(ref[i, c, 0, at], ref[i, c, 1, at]) for c in range(ref.shape[1])]
        for i in range(ref.shape[0])
    ]


def clear_first(acc_ref):
    @pl.when(pl.program_id(0) == 0)
    def _():
        acc_ref[...] = jnp.zeros(acc_ref.shape, acc_ref.dtype)


def block_spec(array, size, dim):
    shape = tuple(size if d == dim else n for d, n in enumerate(array.shape))
    return pl.BlockSpec(shape, lambda s: tuple(s if d == dim else 0 for d in range(array.ndim)))


def acc_out(count, line):
    return jax.ShapeDtypeStruct((count, 8, line), jnp.float32), pl.BlockSpec(
        (count, 8, line), lambda s: (0, 0, 0)
    )


def pick(depth, size):
    return size if depth % size == 0 else 1


def first_gram(block, image):
    bands = block.shape[0]
    step = pick(block.shape[3], 4)
    pairs = 2 * bands * bands

    def kernel(b_ref, m_ref, acc_ref):
        clear_first(acc_ref)

        def one(at, carry):
            left = load_bands(b_ref, at)
            add_pairs(acc_ref, 0, left, left)
            add_pairs(acc_ref, pairs, left, load_bands(m_ref, at))
            return carry

        lax.fori_loop(0, step, one, 0)

    shape, spec = acc_out(2 * pairs, block.shape[5])
    sums = pl.pallas_call(
        kernel,
        grid=(block.shape[3] // step,),
        in_specs=[block_spec(block, step, 3), block_spec(image, step, 3)],
        out_specs=spec,
        out_shape=shape,
        name="first_gram",
    )(block, image)
    return jnp.sum(sums, axis=(1, 2))


def search_gram(block, image, scale, mixing):
    bands = block.shape[0]
    step = pick(block.shape[3], 4)
    pairs = 2 * bands * bands

    def kernel(c_ref, b_ref, m_ref, p_ref, s_ref, acc_ref):
        clear_first(acc_ref)

        def one(at, carry):
            left = load_bands(b_ref, at)
            images = load_bands(m_ref, at)
            factor = p_ref[at]
            search = []
            for j in range(bands):
                parts = []
                for c in range(2):
                    real_part, imag_part = images[j][c]
                    for i in range(bands):
                        br, bi = left[i][c]
                        cr = c_ref[i, j]
                        ci = c_ref[bands + i, j]
                        real_part = real_part - (br * cr - bi * ci)
                        imag_part = imag_part - (br * ci + bi * cr)
                    real_part = real_part * factor
                    imag_part = imag_part * factor
                    s_ref[j, c, 0, at] = real_part
                    s_ref[j, c, 1, at] = imag_part
                    parts.append((real_part, imag_part))
                search.append(parts)
            add_pairs(acc_ref, 0, left, search)
            add_pairs(acc_ref, pairs, search, search)
            add_pairs(acc_ref, 2 * pairs, search, images)
            return carry

        lax.fori_loop(0, step, one, 0)

    shape, spec = acc_out(3 * pairs, block.shape[5])
    search, sums = pl.pallas_call(
        kernel,
        grid=(block.shape[3] // step,),
        in_specs=[
            pl.BlockSpec(memory_space=pltpu.SMEM),
            block_spec(block, step, 3),
            block_spec(image, step, 3),
            block_spec(scale, step, 0),
        ],
        out_specs=[block_spec(block, step, 3), spec],
        out_shape=[jax.ShapeDtypeStruct(block.shape, jnp.float32), shape],
        name="search_gram",
    )(mixing, block, image, scale)
    return search, jnp.sum(sums, axis=(1, 2))


def field_gram(fields, weight):
    bands = fields[0].shape[0]
    depth = fields[0].shape[3]
    step = pick(depth, 4)
    pairs = 2 * bands * bands
    components = len(fields)

    def kernel(*refs):
        e_refs = refs[:components]
        w_ref = refs[components]
        acc_ref = refs[components + 1]
        clear_first(acc_ref)

        def one(at, carry):
            loaded = [load_bands(ref, at) for ref in e_refs]
            right = [sum((part[i] for part in loaded), []) for i in range(bands)]
            factor = w_ref[at]
            left = [[(a * factor, b * factor) for a, b in parts] for parts in right]
            add_pairs(acc_ref, 0, left, right)
            return carry

        lax.fori_loop(0, step, one, 0)

    shape, spec = acc_out(pairs, fields[0].shape[5])
    sums = pl.pallas_call(
        kernel,
        grid=(depth // step,),
        in_specs=[block_spec(f, step, 3) for f in fields] + [block_spec(weight, step, 0)],
        out_specs=spec,
        out_shape=shape,
        name="field_gram",
    )(*fields, weight)
    return jnp.sum(sums, axis=(1, 2))


def solve_small(system, right_side):
    rows = system.shape[0]
    wide = jnp.concatenate([system, right_side], 1)

    def kernel(m_ref, out_ref):
        values = m_ref[...]
        row_index = lax.broadcasted_iota(jnp.int32, values.shape, 0)
        for k in range(rows):
            pivot_row = values[k : k + 1, :] / values[k : k + 1, k : k + 1]
            column = values[:, k : k + 1]
            values = jnp.where(row_index == k, pivot_row, values - column * pivot_row)
        out_ref[...] = values

    solved = pl.pallas_call(
        kernel, out_shape=jax.ShapeDtypeStruct(wide.shape, jnp.float32), name="solve_small"
    )(wide)
    return solved[:, rows:]


def as_pairs(flat, bands):
    pairs = flat.reshape(bands, bands, 2)
    return pairs[:, :, 0], pairs[:, :, 1]


def shards(band_block, material_grid, inverse_permittivity, bloch_index):
    band_groups = lax.axis_size("band")
    slab_count = lax.axis_size("slab")
    band_count = band_block.shape[0]
    depth_share = band_block.shape[3]
    row_share = band_block.shape[4]
    line_length = band_block.shape[5]
    full_depth = depth_share * band_groups
    full_rows = row_share * slab_count
    grid_cells = full_depth * full_rows * line_length
    fraction = (bloch_index[0].astype(jnp.float32) + 1.0) / KPOINTS
    row_offset = lax.axis_index("slab") * row_share
    depth_offset = lax.axis_index("band") * depth_share
    width_wave = axis_values(line_length, 0.5, fraction, 0, line_length)
    row_wave = axis_values(full_rows, 0.35, fraction, row_offset, row_share)
    point_frame = frame(
        axis_values(full_depth, 0.2, fraction, depth_offset, depth_share), row_wave, width_wave
    )
    inverse_cells = cell_values(material_grid, inverse_permittivity, grid_cells)
    line_frame = frame(
        axis_values(full_depth, 0.2, fraction, 0, full_depth), row_wave, width_wave
    )

    def to_space(points, precision=HIGHEST):
        gathered = lax.all_to_all(points, "band", split_axis=0, concat_axis=3, tiled=True)
        fields = []
        for curled in curl_field(gathered, *line_frame):
            spectrum = transform(transform(curled, 2, 1.0, precision), 4, 1.0, precision)
            moved = lax.all_to_all(spectrum, "slab", split_axis=2, concat_axis=3, tiled=True)
            fields.append(transform(moved, 3, 1.0, precision))
        return fields

    def from_space(fields):
        finished = []
        for field in fields:
            returned = lax.all_to_all(
                transform(field * inverse_cells[None, None], 3, -1.0),
                "slab",
                split_axis=3,
                concat_axis=2,
                tiled=True,
            )
            finished.append(transform(transform(returned, 4, -1.0), 2, -1.0))
        local_image = project_back(finished, *line_frame)
        return lax.all_to_all(local_image, "band", split_axis=3, concat_axis=0, tiled=True)

    pair_count = 2 * band_count * band_count
    image = from_space(to_space(band_block))
    sums = lax.psum(first_gram(band_block, image), ("band", "slab")) / grid_cells
    correlation_real, correlation_imag = as_pairs(sums[:pair_count], band_count)
    cross_real, cross_imag = as_pairs(sums[pair_count:], band_count)
    system = jnp.concatenate(
        [
            jnp.concatenate([correlation_real, -correlation_imag], 1),
            jnp.concatenate([correlation_imag, correlation_real], 1),
        ],
        0,
    )
    right_side = jnp.concatenate([cross_real, cross_imag], 0)
    mixing = solve_small(system, right_side)
    magnitude = point_frame[2]
    scale = 1.0 / (magnitude * magnitude + 1.0)
    search_block, search_sums = search_gram(band_block, image, scale, mixing)
    rows_here = full_rows // band_groups
    fields = [
        lax.all_to_all(field[:, None], "band", split_axis=4, concat_axis=0, tiled=True)
        for field in to_space(search_block, HIGH)
    ]
    weight = lax.dynamic_slice_in_dim(
        inverse_cells, lax.axis_index("band") * rows_here, rows_here, 1
    )
    field_sums = field_gram(fields, weight)
    sums = (
        lax.psum(jnp.concatenate([search_sums, field_sums]), ("band", "slab")) / grid_cells
    )
    joint_real, joint_imag = as_pairs(sums[:pair_count], band_count)
    own_real, own_imag = as_pairs(sums[pair_count : 2 * pair_count], band_count)
    back_real, back_imag = as_pairs(sums[2 * pair_count : 3 * pair_count], band_count)
    last_real, last_imag = as_pairs(sums[3 * pair_count :], band_count)
    correlation = jnp.stack(
        [
            jnp.block([[correlation_real, joint_real], [joint_real.T, own_real]]),
            jnp.block([[correlation_imag, joint_imag], [-joint_imag.T, own_imag]]),
        ],
        0,
    )
    projected = jnp.stack(
        [
            jnp.block([[cross_real, back_real.T], [back_real, last_real]]),
            jnp.block([[cross_imag, -back_imag.T], [back_imag, last_imag]]),
        ],
        0,
    )
    return (search_block, correlation, projected)


def solution(mesh):
    return jax.shard_map(
        shards,
        mesh=mesh,
        in_specs=(P(None, None, None, "band", "slab", None), P("slab", None, None), P(), P()),
        out_specs=(P(None, None, None, "band", "slab", None), P(), P()),
        check_vma=False,
    )
```
